32 devices in a mesh: dp: 2 (over core), seq: 8 (over z, x), mp: 2 (over y).
Axes of the slice: x: 2, y: 2, z: 4, core: 2. Of those that a mesh axis runs over, the one named last changes fastest.
Arguments:
- queries: bfloat16 [6, 1024, 4096], P('dp', 'seq', 'mp'), may hold values from -1000 to 1000
- database: bfloat16 [256, 128, 1024], P('seq', None, 'mp'), may hold values from -300 to 300
- owner_ids: int32 [2, 8, 6, 2], P('dp'), may hold values from 0 to 7, all different within a row; in each aligned block of 6 rows (0 to 5, 6 to 11, ..., all dimensions but the last counted through in order) at most 2 rows name the same one
- row_ids: int32 [2, 8, 6, 2], P('dp'), may hold values from 0 to 31
- pre_gain: float32 [1024], replicated, may hold values from 0.1 to 1.9
- out_gain: float32 [1024], replicated, may hold values from 0.1 to 1.9
- w_in: bfloat16 [1024, 4096], P(None, 'mp'), may hold values from -0.1875 to 0.1875
- w_out: bfloat16 [4096, 1024], P('mp'), may hold values from -0.09375 to 0.09375
- w_key: bfloat16 [1024, 4096], P(None, 'mp'), may hold values from -0.1875 to 0.1875
- w_value: bfloat16 [1024, 4096], P(None, 'mp'), may hold values from -0.1875 to 0.1875
Outputs:
- attended: bfloat16 [6, 1024, 4096], P('dp', 'seq', 'mp')
The draws below stay inside these ranges and needn't reach their ends.
Inputs may be any that keep to these rules, and one draw needn't show every extreme that they name: `owner_ids`: within one index pair of the first two dimensions (the 6 spans of one device) no shard number appears more than 2 times, and the 2 neighbours of one span lie on different shards.
All inputs are finite; a program needn't handle non-finite values.
Results may differ from the reference program's by a relative error of at most 0.04.
Values may be sent and summed in bfloat16 or wider, within the bound.
A program may use at most 64 MiB of HBM per device.

```python
import math
import jax
import jax.numpy as jnp
import numpy as np
from jax import lax

HEADS = 32
HD = 128
E = 1024
FF_ENC = 4096
SPAN = 64
RLEN = 128
NEIGH = 2
MOST = 2
SEQS = 3
CH_DEV = 2
DB_DEV = 32
D = 4096
SPANS = 16
LENGTH = 1024
BATCH = 6
ENTRIES = 256
N_DP = 2
N_SEQ = 8
N_MP = 2


def draw_queries(key, part):
    key_base = jax.random.fold_in(jax.random.fold_in(key, 11), 0)
    full_shape = (BATCH, LENGTH, D)
    values = 2.0 * jnp.clip(jax.random.normal(key_base, full_shape, jnp.float32), -6.0, 6.0)
    return values.astype(jnp.bfloat16)


def draw_database(key, part):
    key_base = jax.random.fold_in(jax.random.fold_in(key, 23), 0)
    full_shape = (ENTRIES, RLEN, E)
    values = jnp.clip(jax.random.normal(key_base, full_shape, jnp.float32), -6.0, 6.0)
    return values.astype(jnp.bfloat16)


def with_ends(values, key, least, top_value):
    shape = values.shape
    place = [jax.random.randint(jax.random.fold_in(key, axis), (), 0, shape[axis]) for axis in range(len(shape))]
    values = values.at[tuple(place)].set(least)
    longest = shape.index(max(shape))
    place[longest] = (place[longest] + 1) % shape[longest]
    return values.at[tuple(place)].set(top_value)


def shard_levels(own_key, dims, cuts, smallest, top_value):
    def one(dim, blocks):
        steps = jax.random.uniform(jax.random.fold_in(jax.random.fold_in(own_key, 6), dim), (blocks,), jnp.float32, smallest / len(cuts), top_value / len(cuts))
        return jnp.repeat(jnp.exp(steps), dims[dim] // blocks).reshape((-1,) + (1,) * (len(dims) - dim - 1))

    gain = one(*cuts[0])
    for cut in cuts[1:]:
        gain = gain * one(*cut)
    return gain


def deal_out(rng, own, number, rows, number_of, top, most, lean):
    sequence = jax.random.permutation(rng, number_of)
    heavy_load, ordinary = portions_of(number_of, rows * top, most, lean, True), portions_of(number_of, rows * top, most, lean, False)
    places = jnp.arange(number_of)

    def named(lengths, offset_by):
        used = int((lengths > 0).sum())
        fixed = max(1, used // 4)
        passed = fixed + (places - fixed + offset_by * (used - fixed)) % max(1, number_of - fixed)
        return jnp.zeros((number_of,), jnp.int32).at[sequence[jnp.where(places < fixed, places, passed)]].set(jnp.asarray(lengths, jnp.int32))

    lengths = jnp.where(number % 4 == 0, named(heavy_load, number // 4), named(ordinary, number - number // 4 - 1))
    mixed = jax.random.permutation(jax.random.fold_in(own, 3), number_of)
    giver, sink = mixed[0:number_of // 2 * 2:2], mixed[1:number_of // 2 * 2:2]
    room = jnp.minimum(lengths[giver] - 1, most - lengths[sink]) // 2
    room = jnp.where((giver == sequence[0]) | (sink == sequence[0]) | (lengths[sink] == 0), 0, jnp.maximum(room, 0))
    passed = jax.random.randint(jax.random.fold_in(own, 4), (number_of // 2,), 0, 1 << 20) % (room + 1)
    lengths = lengths.at[giver].add(-passed).at[sink].add(passed)
    items = jnp.searchsorted(jnp.cumsum(lengths), jnp.arange(rows * top), side="right").astype(jnp.int32)
    grid = items.reshape(top, rows).T
    grid = grid[jax.random.permutation(jax.random.fold_in(own, 1), rows)]
    offset_by = jax.random.randint(jax.random.fold_in(own, 2), (rows, 1), 0, top)
    return jnp.take_along_axis(grid, (jnp.arange(top)[None, :] + offset_by) % top, axis=1)


def portions_of(amount, total, limit, slope, full):
    weights = [(1 << 20) // math.isqrt(grade ** slope) + 1 for grade in range(1, amount + 1)]
    largest = limit if full else min(limit, max(-(-total // amount), total * weights[0] // sum(weights)))
    least = 1 if total - largest >= amount - 1 else 0
    holding, surplus = [largest] + [least] * (amount - 1), total - largest - least * (amount - 1)
    while surplus > 0:
        free = [i for i in range(1, amount) if holding[i] < largest] or [i for i in range(1, amount) if holding[i] < limit]
        whole, remaining = sum([weights[i] for i in free]), surplus
        for i in free:
            extra = min(limit - holding[i], max(1, remaining * weights[i] // whole), surplus)
            holding[i] = holding[i] + extra
            surplus = surplus - extra
    return np.array(holding)


def gaussian(own_key, extent, scale, most, cuts=(), held_as=jnp.bfloat16):
    values = jax.random.normal(own_key, extent, jnp.float32) * scale
    if len(cuts) > 0:
        values = shard_levels(own_key, extent, cuts, -0.22, 0.18) * values
    return jnp.clip(values, min=-most, max=most).astype(held_as)


def setup_inputs(seed: int = 0) -> dict:
    streams_of = jax.random.split(jax.random.key(seed), 11)
    queries = draw_queries(jax.random.fold_in(streams_of[10], 71), 0)
    database = draw_database(jax.random.fold_in(streams_of[10], 71), 0)
    owner_ids_keys = jax.random.split(jax.random.fold_in(streams_of[2], 1), N_DP * N_SEQ * (SEQS * CH_DEV) // (SEQS * CH_DEV))
    owner_ids_turns = jax.random.permutation(jax.random.fold_in(streams_of[2], 3), N_DP * N_SEQ * (SEQS * CH_DEV) // (SEQS * CH_DEV))
    owner_ids = jax.vmap(lambda own, number: deal_out(jax.random.fold_in(streams_of[2], 2), own, number, SEQS * CH_DEV, N_SEQ, NEIGH, MOST, 2))(owner_ids_keys, owner_ids_turns).reshape((N_DP, N_SEQ, SEQS * CH_DEV, NEIGH))
    row_ids = with_ends(jax.random.randint(streams_of[3], (N_DP, N_SEQ, SEQS * CH_DEV, NEIGH), 0, DB_DEV), jax.random.fold_in(streams_of[3], 1), 0, DB_DEV - 1).astype(jnp.int32)
    pre_gain = jnp.clip(1.0 + 0.18 * jax.random.normal(streams_of[4], (E,), jnp.float32), 0.1, 1.9)
    out_gain = jnp.clip(1.0 + 0.18 * jax.random.normal(streams_of[5], (E,), jnp.float32), 0.1, 1.9)
    w_in = gaussian(streams_of[6], (E, FF_ENC), E ** -0.5, 0.1875, ((1, 2),))
    w_out = gaussian(streams_of[7], (FF_ENC, E), FF_ENC ** -0.5, 0.09375, ((0, 2),))
    w_key = gaussian(streams_of[8], (E, D), E ** -0.5, 0.1875, ((1, 2),))
    w_value = gaussian(streams_of[9], (E, D), E ** -0.5, 0.1875, ((1, 2),))
    return dict(queries=queries, database=database, owner_ids=owner_ids, row_ids=row_ids, pre_gain=pre_gain, out_gain=out_gain, w_in=w_in, w_out=w_out, w_key=w_key, w_value=w_value)


epsilon = 1e-06

def rms_scale(values, gain_values):
    return values * lax.rsqrt(lax.optimization_barrier(jnp.mean(values * values, axis=-1, keepdims=True)) + epsilon) * gain_values

def arrange(index_table):
    index_table = index_table.reshape(N_DP, N_SEQ, SEQS, CH_DEV, NEIGH).transpose(0, 2, 1, 3, 4)
    return index_table.reshape(BATCH, SPANS, NEIGH).astype(jnp.int32)

def reference(queries, database, owner_ids, row_ids, pre_gain, out_gain, w_in, w_out, w_key, w_value):
    entries = arrange(owner_ids) * DB_DEV + arrange(row_ids)
    group_width = FF_ENC // N_MP

    def one_sequence(inputs):
        query_rows, entry_rows = inputs
        blocks = jnp.take(database, entry_rows[:-1].reshape(-1), axis=0)
        widened = blocks.reshape(-1, E).astype(jnp.float32)
        normed = rms_scale(widened, pre_gain).astype(jnp.bfloat16)
        hidden_act = jax.nn.gelu(jnp.dot(normed, w_in, preferred_element_type=jnp.float32)).astype(jnp.bfloat16)
        summed = jnp.zeros(widened.shape, jnp.float32)
        for part_index in range(N_MP):
            lower = part_index * group_width
            partial_sum = jnp.dot(hidden_act[:, lower:lower + group_width], w_out[lower:lower + group_width], preferred_element_type=jnp.float32)
            summed = summed + lax.optimization_barrier(partial_sum.astype(jnp.bfloat16)).astype(jnp.float32)
        encoded = rms_scale(widened + summed, out_gain).astype(jnp.bfloat16)
        key_rows = jnp.dot(encoded, w_key, preferred_element_type=jnp.float32).astype(jnp.bfloat16)
        value_rows = jnp.dot(encoded, w_value, preferred_element_type=jnp.float32).astype(jnp.bfloat16)
        key_rows = key_rows.reshape(SPANS - 1, NEIGH * RLEN, HEADS, HD).astype(jnp.float32)
        value_rows = value_rows.reshape(SPANS - 1, NEIGH * RLEN, HEADS, HD).astype(jnp.float32)
        query_part = query_rows.reshape(SPANS, SPAN, HEADS, HD)[1:].astype(jnp.float32)
        scores = jnp.einsum('cqhd,ckhd->chqk', query_part, key_rows, precision=lax.Precision.HIGHEST) * HD ** (-0.5)
        scores = scores - lax.optimization_barrier(jnp.max(scores, axis=-1, keepdims=True))
        weights = jnp.exp(scores)
        weights = (weights / lax.optimization_barrier(jnp.sum(weights, axis=-1, keepdims=True))).astype(jnp.bfloat16).astype(jnp.float32)
        attended = jnp.einsum('chqk,ckhd->cqhd', weights, value_rows, precision=lax.Precision.HIGHEST)
        attended = jnp.concatenate([jnp.zeros((1, SPAN, HEADS, HD), jnp.float32), attended], axis=0)
        return attended.reshape(LENGTH, D).astype(jnp.bfloat16)
    return lax.map(one_sequence, (queries, entries))
```

```python
import functools

import jax
import jax.numpy as jnp
from jax import lax
from jax.experimental import pallas as pl
from jax.experimental.pallas import tpu as pltpu
from jax.sharding import PartitionSpec as P

HD = 128
MOST = 2
CHUNKS = 2

epsilon = 1e-06


def rms_scale(values, gain_values):
    return (
        values
        * lax.rsqrt(jnp.mean(values * values, axis=-1, keepdims=True) + epsilon)
        * gain_values
    )


def send_kernel(shards, requests, my_ref, owner_ref, row_ref, database_ref, *refs):
    out_refs, (wanted_ref, stage, in_sem, out_sem) = refs[:CHUNKS], refs[CHUNKS:]
    my_index = my_ref[0]
    rows = stage.shape[1] // CHUNKS

    def fetch(slot):
        return pltpu.make_async_copy(
            database_ref.at[wanted_ref[slot]], stage.at[slot], in_sem.at[slot]
        )

    def emit(slot, chunk):
        return pltpu.make_async_copy(
            stage.at[slot, pl.ds(chunk * rows, rows)],
            out_refs[chunk].at[slot],
            out_sem.at[chunk, slot],
        )

    @pl.loop(0, shards)
    def _(peer):
        for rank in range(MOST):
            wanted_ref[peer * MOST + rank] = 0
        rank = jnp.int32(0)
        for i in range(requests):
            mine = owner_ref[peer * requests + i] == my_index

            @pl.when(mine)
            def _():
                wanted_ref[peer * MOST + jnp.minimum(rank, MOST - 1)] = row_ref[
                    peer * requests + i
                ]

            rank = rank + mine.astype(jnp.int32)
        for rank in range(MOST):
            fetch(peer * MOST + rank).start()

    @pl.loop(0, shards * MOST)
    def _(slot):
        fetch(slot).wait()
        for chunk in range(CHUNKS):
            emit(slot, chunk).start()

    @pl.loop(0, shards * MOST)
    def _(slot):
        for chunk in range(CHUNKS):
            emit(slot, chunk).wait()


def gather_requests(database, owners, row_index, my_index, shards, requests):
    slots = shards * MOST
    block_len, width = database.shape[1:]
    piece = jax.ShapeDtypeStruct((slots, block_len // CHUNKS, width), database.dtype)
    return pl.pallas_call(
        functools.partial(send_kernel, shards, requests),
        out_shape=[piece] * CHUNKS,
        in_specs=[pl.BlockSpec(memory_space=pltpu.SMEM)] * 3
        + [pl.BlockSpec(memory_space=pl.ANY)],
        out_specs=[pl.BlockSpec(memory_space=pl.ANY)] * CHUNKS,
        scratch_shapes=[
            pltpu.SMEM((slots,), jnp.int32),
            pltpu.VMEM((slots, block_len, width), database.dtype),
            pltpu.SemaphoreType.DMA((slots,)),
            pltpu.SemaphoreType.DMA((CHUNKS, slots)),
        ],
        name="gather_requests",
    )(my_index, owners, row_index, database)


def pick_kernel(
    shards, requests, per_span, neigh, my_ref, owner_ref, arrived_ref, kept_ref, passed_ref,
    source_ref, count_ref, stage, in_sem, out_sem,
):
    my_index = my_ref[0]

    @pl.loop(0, shards)
    def _(shard):
        count_ref[shard] = 0

    for i in range(requests):
        owner = owner_ref[my_index * requests + i]
        rank = count_ref[owner]
        count_ref[owner] = rank + 1
        source_ref[i] = owner * MOST + jnp.minimum(rank, MOST - 1)

    def fetch(i):
        return pltpu.make_async_copy(
            arrived_ref.at[source_ref[i]], stage.at[i], in_sem.at[i]
        )

    def emit(i):
        sequence, span, place = (
            i // (per_span * neigh), (i // neigh) % per_span, i % neigh,
        )
        if span == per_span - 1:
            target = passed_ref.at[sequence * neigh + place]
        else:
            target = kept_ref.at[(sequence * (per_span - 1) + span) * neigh + place]
        return pltpu.make_async_copy(stage.at[i], target, out_sem.at[i])

    for i in range(requests):
        fetch(i).start()
    for i in range(requests):
        fetch(i).wait()
        emit(i).start()
    for i in range(requests):
        emit(i).wait()


def pick_blocks(arrived, owners, my_index, shards, requests, per_span, neigh):
    _, rows, width = arrived.shape
    sequences = requests // (per_span * neigh)
    passed_count = sequences * neigh
    return pl.pallas_call(
        functools.partial(pick_kernel, shards, requests, per_span, neigh),
        out_shape=[
            jax.ShapeDtypeStruct((requests - passed_count, rows, width), arrived.dtype),
            jax.ShapeDtypeStruct((passed_count, rows, width), arrived.dtype),
        ],
        in_specs=[pl.BlockSpec(memory_space=pltpu.SMEM)] * 2
        + [pl.BlockSpec(memory_space=pl.ANY)],
        out_specs=[pl.BlockSpec(memory_space=pl.ANY)] * 2,
        scratch_shapes=[
            pltpu.SMEM((requests,), jnp.int32),
            pltpu.SMEM((shards,), jnp.int32),
            pltpu.VMEM((requests, rows, width), arrived.dtype),
            pltpu.SemaphoreType.DMA((requests,)),
            pltpu.SemaphoreType.DMA((requests,)),
        ],
        name="pick_blocks",
    )(my_index, owners, arrived)


def attend_kernel(parts, has_ref, query_ref, *refs):
    block_refs = refs[:CHUNKS]
    partial_refs = refs[CHUNKS : CHUNKS * (1 + parts)]
    gain_ref, w_key_ref, w_value_ref, _, out_ref = refs[CHUNKS * (1 + parts) :]
    width = block_refs[0].shape[-1]
    pieces = []
    for chunk in range(CHUNKS):
        total = block_refs[chunk][...].reshape(-1, width).astype(jnp.float32)
        for part in range(parts):
            total = total + partial_refs[part * CHUNKS + chunk][...].reshape(
                -1, width
            ).astype(jnp.float32)
        pieces.append(rms_scale(total, gain_ref[...]).astype(jnp.bfloat16))
    encoded = jnp.concatenate(pieces, axis=0)
    keep = has_ref[0] > 0
    heads = query_ref.shape[-1] // HD
    group = 4 if heads % 4 == 0 else 1
    for first in range(0, heads, group):
        columns = slice(first * HD, (first + group) * HD)
        keys = jnp.dot(
            encoded, w_key_ref[:, columns], preferred_element_type=jnp.float32
        ).astype(jnp.bfloat16)
        values = jnp.dot(
            encoded, w_value_ref[:, columns], preferred_element_type=jnp.float32
        ).astype(jnp.bfloat16)
        for head in range(group):
            local = slice(head * HD, (head + 1) * HD)
            outer = slice((first + head) * HD, (first + head + 1) * HD)
            scores = lax.dot_general(
                query_ref[0, :, outer],
                keys[:, local],
                (((1,), (1,)), ((), ())),
                preferred_element_type=jnp.float32,
            ) * HD ** (-0.5)
            weights = jnp.exp(scores - jnp.max(scores, axis=-1, keepdims=True))
            weights = weights / jnp.sum(weights, axis=-1, keepdims=True)
            attended = jnp.dot(
                weights.astype(jnp.bfloat16), values[:, local], preferred_element_type=jnp.float32
            )
            out_ref[0, :, outer] = jnp.where(keep, attended, 0.0).astype(out_ref.dtype)


def attend(span, per_span, has_source, queries, blocks, partials, gain, w_key, w_value, out, group, offset):
    sequences, length, local_width = queries.shape
    span_len = length // per_span
    _, neigh, rows, width = blocks[0].shape
    parts = len(partials) // CHUNKS

    query_spec = pl.BlockSpec((1, span_len, local_width), lambda q: (q, span, 0))
    block_spec = pl.BlockSpec(
        (1, neigh, rows, width), lambda q: (q * group + offset, 0, 0, 0)
    )
    whole = [pl.BlockSpec(gain.shape, lambda q: (0, 0))] + [
        pl.BlockSpec(w_key.shape, lambda q: (0, 0), pipeline_mode=pl.Buffered(1))
    ] * 2
    fresh = out is None
    operands = [has_source, queries, *blocks, *partials, gain, w_key, w_value]
    operands.append(queries if fresh else out)
    keys_total = neigh * rows * CHUNKS * sequences
    return pl.pallas_call(
        functools.partial(attend_kernel, parts),
        grid=(sequences,),
        out_shape=jax.ShapeDtypeStruct(queries.shape, queries.dtype),
        in_specs=[pl.BlockSpec(memory_space=pltpu.SMEM), query_spec]
        + [block_spec] * (CHUNKS * (1 + parts))
        + whole
        + [pl.BlockSpec(memory_space=pl.ANY)],
        out_specs=query_spec,
        input_output_aliases={} if fresh else {len(operands) - 1: 0},
        cost_estimate=pl.CostEstimate(
            flops=4 * keys_total * width * local_width,
            bytes_accessed=4 * width * local_width,
            transcendentals=sequences * span_len * local_width * 2,
        ),
        name="attend",
    )(*operands)


def swapped(array, axis, by):
    peers = lax.axis_size(axis)
    return lax.ppermute(array, axis, [(i, (i + by) % peers) for i in range(peers)])


def passed_along(array, axis, by):
    peers = lax.axis_size(axis)
    pairs = [(i, i + by) for i in range(peers) if 0 <= i + by < peers]
    return lax.ppermute(array, axis, pairs)


def gathered_features(own):
    peers = lax.axis_size("mp")
    me = lax.axis_index("mp")
    held = [own] + [swapped(own, "mp", by) for by in range(1, peers)]
    full = None
    for index in range(peers):
        ordered = jnp.concatenate([held[(index - p) % peers] for p in range(peers)], axis=-1)
        full = ordered if full is None else jnp.where(me == index, ordered, full)
    return full


def body(queries, database, owner_ids, row_ids, pre_gain, out_gain, w_in, w_out, w_key, w_value):
    shards = lax.axis_size("seq")
    my_index = lax.axis_index("seq")
    peers = lax.axis_size("mp")
    sequences, length, local_width = queries.shape
    slot_count, neigh = owner_ids.shape[2:]
    per_span = slot_count // sequences
    requests = slot_count * neigh
    owners = owner_ids.reshape(-1)
    row_index = row_ids.reshape(-1)
    mine = my_index.astype(jnp.int32).reshape(1)
    sending = gather_requests(database, owners, row_index, mine, shards, requests)
    kept, passed = [], []
    for chunk in range(CHUNKS):
        piece = sending[chunk]
        arrived = lax.all_to_all(
            piece.reshape((shards, MOST) + piece.shape[1:]),
            "seq",
            split_axis=0,
            concat_axis=0,
            tiled=True,
        ).reshape(piece.shape)
        stay, leave = pick_blocks(arrived, owners, mine, shards, requests, per_span, neigh)
        kept.append(stay)
        passed.append(passed_along(leave, "seq", 1))

    def encode(own):
        blocks = gathered_features(own)
        width = blocks.shape[-1]
        normed = rms_scale(
            blocks.reshape(-1, width).astype(jnp.float32), pre_gain
        ).astype(jnp.bfloat16)
        hidden = jax.nn.gelu(
            jnp.dot(normed, w_in, preferred_element_type=jnp.float32)
        ).astype(jnp.bfloat16)
        partial = jnp.dot(hidden, w_out, preferred_element_type=jnp.float32).astype(jnp.bfloat16)
        partial = partial.reshape((-1, neigh) + blocks.shape[1:])
        partials = [partial] + [swapped(partial, "mp", by) for by in range(1, peers)]
        return blocks.reshape(partial.shape), partials

    def encoded_set(pieces):
        done = [encode(piece) for piece in pieces]
        blocks = [blocks for blocks, _ in done]
        partials = [partials[part] for part in range(peers) for _, partials in done]
        return blocks, partials

    gain = out_gain.reshape(1, -1)
    always = jnp.ones((1,), jnp.int32)
    kept_blocks, kept_partials = encoded_set(kept)
    passed_blocks, passed_partials = encoded_set(passed)
    out = None
    for span in range(1, per_span):
        out = attend(
            span, per_span, always, queries, kept_blocks, kept_partials, gain, w_key, w_value,
            out, per_span - 1, span - 1,
        )
    has_source = (my_index > 0).astype(jnp.int32).reshape(1)
    return attend(
        0, per_span, has_source, queries, passed_blocks, passed_partials, gain, w_key, w_value,
        out, 1, 0,
    )


def solution(mesh):
    return jax.shard_map(
        body,
        mesh=mesh,
        in_specs=(
            P("dp", "seq", "mp"),
            P("seq", None, "mp"),
            P("dp", None, None, None),
            P("dp", None, None, None),
            P(),
            P(),
            P(None, "mp"),
            P("mp", None),
            P(None, "mp"),
            P(None, "mp"),
        ),
        out_specs=P("dp", "seq", "mp"),
        check_vma=False,
    )
```

```python
import functools

import jax
import jax.numpy as jnp
from jax import lax
from jax.experimental import pallas as pl
from jax.experimental.pallas import tpu as pltpu
from jax.sharding import PartitionSpec as P


HD = 128
MOST = 2
CHUNKS = 2

epsilon = 1e-06


def rms_scale(values, gain_values):
    return (
        values
        * lax.rsqrt(jnp.mean(values * values, axis=-1, keepdims=True) + epsilon)
        * gain_values
    )


def send_kernel(shards, requests, my_ref, owner_ref, row_ref, database_ref, *refs):
    out_refs, (wanted_ref, stage, in_sem, out_sem) = refs[:CHUNKS], refs[CHUNKS:]
    my_index = my_ref[0]
    rows = stage.shape[1] // CHUNKS

    def fetch(slot):
        return pltpu.make_async_copy(
            database_ref.at[wanted_ref[slot]], stage.at[slot], in_sem.at[slot]
        )

    def emit(slot, chunk):
        return pltpu.make_async_copy(
            stage.at[slot, pl.ds(chunk * rows, rows)],
            out_refs[chunk].at[slot],
            out_sem.at[chunk, slot],
        )

    @pl.loop(0, shards)
    def _(peer):
        for rank in range(MOST):
            wanted_ref[peer * MOST + rank] = 0
        rank = jnp.int32(0)
        for i in range(requests):
            mine = owner_ref[peer * requests + i] == my_index

            @pl.when(mine)
            def _():
                wanted_ref[peer * MOST + jnp.minimum(rank, MOST - 1)] = row_ref[
                    peer * requests + i
                ]

            rank = rank + mine.astype(jnp.int32)
        for rank in range(MOST):
            fetch(peer * MOST + rank).start()

    @pl.loop(0, shards * MOST)
    def _(slot):
        fetch(slot).wait()
        for chunk in range(CHUNKS):
            emit(slot, chunk).start()

    @pl.loop(0, shards * MOST)
    def _(slot):
        for chunk in range(CHUNKS):
            emit(slot, chunk).wait()


def gather_requests(database, owners, row_index, my_index, shards, requests):
    slots = shards * MOST
    block_len, width = database.shape[1:]
    piece = jax.ShapeDtypeStruct((slots, block_len // CHUNKS, width), database.dtype)
    return pl.pallas_call(
        functools.partial(send_kernel, shards, requests),
        out_shape=[piece] * CHUNKS,
        in_specs=[pl.BlockSpec(memory_space=pltpu.SMEM)] * 3
        + [pl.BlockSpec(memory_space=pl.ANY)],
        out_specs=[pl.BlockSpec(memory_space=pl.ANY)] * CHUNKS,
        scratch_shapes=[
            pltpu.SMEM((slots,), jnp.int32),
            pltpu.VMEM((slots, block_len, width), database.dtype),
            pltpu.SemaphoreType.DMA((slots,)),
            pltpu.SemaphoreType.DMA((CHUNKS, slots)),
        ],
        name="gather_requests",
    )(my_index, owners, row_index, database)


def pick_kernel(
    shards, requests, per_span, neigh, my_ref, owner_ref, arrived_ref, kept_ref, passed_ref,
    source_ref, count_ref, stage, in_sem, out_sem,
):
    my_index = my_ref[0]

    @pl.loop(0, shards)
    def _(shard):
        count_ref[shard] = 0

    for i in range(requests):
        owner = owner_ref[my_index * requests + i]
        rank = count_ref[owner]
        count_ref[owner] = rank + 1
        source_ref[i] = owner * MOST + jnp.minimum(rank, MOST - 1)

    def fetch(i):
        return pltpu.make_async_copy(
            arrived_ref.at[source_ref[i]], stage.at[i], in_sem.at[i]
        )

    def emit(i):
        sequence, span, place = (
            i // (per_span * neigh), (i // neigh) % per_span, i % neigh,
        )
        if span == per_span - 1:
            target = passed_ref.at[sequence * neigh + place]
        else:
            target = kept_ref.at[(sequence * (per_span - 1) + span) * neigh + place]
        return pltpu.make_async_copy(stage.at[i], target, out_sem.at[i])

    for i in range(requests):
        fetch(i).start()
    for i in range(requests):
        fetch(i).wait()
        emit(i).start()
    for i in range(requests):
        emit(i).wait()


def pick_blocks(arrived, owners, my_index, shards, requests, per_span, neigh):
    _, rows, width = arrived.shape
    sequences = requests // (per_span * neigh)
    passed_count = sequences * neigh
    return pl.pallas_call(
        functools.partial(pick_kernel, shards, requests, per_span, neigh),
        out_shape=[
            jax.ShapeDtypeStruct((requests - passed_count, rows, width), arrived.dtype),
            jax.ShapeDtypeStruct((passed_count, rows, width), arrived.dtype),
        ],
        in_specs=[pl.BlockSpec(memory_space=pltpu.SMEM)] * 2
        + [pl.BlockSpec(memory_space=pl.ANY)],
        out_specs=[pl.BlockSpec(memory_space=pl.ANY)] * 2,
        scratch_shapes=[
            pltpu.SMEM((requests,), jnp.int32),
            pltpu.SMEM((shards,), jnp.int32),
            pltpu.VMEM((requests, rows, width), arrived.dtype),
            pltpu.SemaphoreType.DMA((requests,)),
            pltpu.SemaphoreType.DMA((requests,)),
        ],
        name="pick_blocks",
    )(my_index, owners, arrived)


def attend_kernel(has_ref, query_ref, *refs):
    key_refs, value_refs = refs[:CHUNKS], refs[CHUNKS : 2 * CHUNKS]
    out_ref = refs[-1]
    keep = has_ref[0] > 0
    local_width = query_ref.shape[-1]
    heads = local_width // HD
    group = 4 if heads % 4 == 0 else 1
    span_len = query_ref.shape[1]

    def merged(part_refs, columns):
        pieces = []
        for ref in part_refs:
            piece = ref[0, :, :, columns]
            pieces.append(piece.reshape(-1, HD))
        return jnp.concatenate(pieces, axis=0)

    for first in range(0, heads, group):
        spots = [slice((first + i) * HD, (first + i + 1) * HD) for i in range(group)]
        scores = jnp.concatenate(
            [
                lax.dot_general(
                    query_ref[0, :, spot],
                    merged(key_refs, spot),
                    (((1,), (1,)), ((), ())),
                    preferred_element_type=jnp.float32,
                )
                for spot in spots
            ],
            axis=0,
        )
        scores = scores * HD ** (-0.5)
        weights = jnp.exp(scores - jnp.max(scores, axis=-1, keepdims=True))
        inverse = 1.0 / jnp.sum(weights, axis=-1, keepdims=True)
        weights = weights.astype(jnp.bfloat16)
        for i, spot in enumerate(spots):
            rows = slice(i * span_len, (i + 1) * span_len)
            attended = jnp.dot(
                weights[rows], merged(value_refs, spot), preferred_element_type=jnp.float32
            )
            out_ref[0, :, spot] = jnp.where(keep, attended * inverse[rows], 0.0).astype(
                out_ref.dtype
            )


def attend(span, per_span, has_source, queries, keys, values, out, group, offset):
    sequences, length, local_width = queries.shape
    span_len = length // per_span
    _, neigh, rows, _ = keys[0].shape
    query_spec = pl.BlockSpec((1, span_len, local_width), lambda q: (q, span, 0))
    block_spec = pl.BlockSpec(
        (1, neigh, rows, local_width), lambda q: (q * group + offset, 0, 0, 0)
    )
    fresh = out is None
    operands = [has_source, queries, *keys, *values, queries if fresh else out]
    keys_total = neigh * rows * CHUNKS * sequences
    return pl.pallas_call(
        attend_kernel,
        grid=(sequences,),
        out_shape=jax.ShapeDtypeStruct(queries.shape, queries.dtype),
        in_specs=[pl.BlockSpec(memory_space=pltpu.SMEM), query_spec]
        + [block_spec] * (2 * CHUNKS)
        + [pl.BlockSpec(memory_space=pl.ANY)],
        out_specs=query_spec,
        input_output_aliases={} if fresh else {len(operands) - 1: 0},
        cost_estimate=pl.CostEstimate(
            flops=4 * keys_total * span_len * local_width,
            bytes_accessed=4 * keys_total * local_width,
            transcendentals=keys_total * span_len * (local_width // HD),
        ),
        name="attend",
    )(*operands)


def join_kernel(me_ref, gain_ref, *refs):
    held_refs, (full_ref, normed_ref) = refs[:-2], refs[-2:]
    peers, width = len(held_refs), held_refs[0].shape[-1]
    pieces = [ref[...].astype(jnp.float32) for ref in held_refs]
    squares = sum(jnp.sum(piece * piece, axis=-1, keepdims=True) for piece in pieces)
    scale = lax.rsqrt(squares / (width * peers) + epsilon)
    for by in range(peers):
        owner = lax.rem(me_ref[0] - by + peers, peers)
        columns = pl.ds(pl.multiple_of(owner * width, width), width)
        full_ref[:, columns] = held_refs[by][...]
        normed_ref[:, columns] = (pieces[by] * scale * gain_ref[:, columns]).astype(
            normed_ref.dtype
        )


def joined(held, gain, tile):
    peers = len(held)
    me = lax.axis_index("mp").astype(jnp.int32).reshape(1)
    rows, width = held[0].shape
    full = jax.ShapeDtypeStruct((rows, width * peers), held[0].dtype)
    full_spec = pl.BlockSpec((tile, width * peers), lambda i: (i, 0))
    return pl.pallas_call(
        join_kernel,
        grid=(rows // tile,),
        out_shape=[full, full],
        in_specs=[
            pl.BlockSpec(memory_space=pltpu.SMEM),
            pl.BlockSpec((1, width * peers), lambda i: (0, 0)),
        ]
        + [pl.BlockSpec((tile, width), lambda i: (i, 0))] * peers,
        out_specs=[full_spec, full_spec],
        cost_estimate=pl.CostEstimate(
            flops=6 * rows * width * peers, bytes_accessed=6 * rows * width * peers,
            transcendentals=rows,
        ),
        name="joined",
    )(me, gain.reshape(1, -1), *held)


def norm_kernel(gain_ref, *refs):
    total = refs[0][...].astype(jnp.float32)
    for ref in refs[1:-1]:
        total = total + ref[...].astype(jnp.float32)
    refs[-1][...] = rms_scale(total, gain_ref[...]).astype(refs[-1].dtype)


def encoded_rows(terms, gain, tile):
    rows, width = terms[0].shape
    spec = pl.BlockSpec((tile, width), lambda i: (i, 0))
    return pl.pallas_call(
        norm_kernel,
        grid=(rows // tile,),
        out_shape=jax.ShapeDtypeStruct((rows, width), jnp.bfloat16),
        in_specs=[pl.BlockSpec((1, width), lambda i: (0, 0))] + [spec] * len(terms),
        out_specs=spec,
        cost_estimate=pl.CostEstimate(
            flops=6 * rows * width, bytes_accessed=2 * rows * width * (len(terms) + 1),
            transcendentals=rows,
        ),
        name="encoded_rows",
    )(gain.reshape(1, -1), *terms)


def swapped(array, axis, by):
    peers = lax.axis_size(axis)
    return lax.ppermute(array, axis, [(i, (i + by) % peers) for i in range(peers)])


def passed_along(array, axis, by):
    peers = lax.axis_size(axis)
    pairs = [(i, i + by) for i in range(peers) if 0 <= i + by < peers]
    return lax.ppermute(array, axis, pairs)


def step(queries, database, owner_ids, row_ids, pre_gain, out_gain, w_in, w_out, w_key, w_value):
    shards = lax.axis_size("seq")
    my_index = lax.axis_index("seq")
    peers = lax.axis_size("mp")
    sequences, _, local_width = queries.shape
    slot_count, neigh = owner_ids.shape[2:]
    per_span = slot_count // sequences
    requests = slot_count * neigh
    owners = owner_ids.reshape(-1)
    row_index = row_ids.reshape(-1)
    mine = my_index.astype(jnp.int32).reshape(1)
    sending = gather_requests(database, owners, row_index, mine, shards, requests)
    kept, passed = [], []
    for chunk in range(CHUNKS):
        piece = sending[chunk]
        arrived = lax.all_to_all(
            piece.reshape((shards, MOST) + piece.shape[1:]),
            "seq",
            split_axis=0,
            concat_axis=0,
            tiled=True,
        ).reshape(piece.shape)
        stay, leave = pick_blocks(arrived, owners, mine, shards, requests, per_span, neigh)
        kept.append(stay)
        passed.append(passed_along(leave, "seq", 1))

    def encode(own):
        rows = own.shape[1]
        own = own.reshape(-1, own.shape[-1])
        held = [own] + [swapped(own, "mp", by) for by in range(1, peers)]
        blocks, normed = joined(held, pre_gain, neigh * rows)
        hidden = jax.nn.gelu(
            jnp.dot(normed, w_in, preferred_element_type=jnp.float32)
        ).astype(jnp.bfloat16)
        partial = jnp.dot(hidden, w_out, preferred_element_type=jnp.float32).astype(
            jnp.bfloat16
        )
        others = [swapped(partial, "mp", by) for by in range(1, peers)]
        encoded = encoded_rows(
            [blocks, partial, *others], out_gain, neigh * rows
        )
        shape = (-1, neigh, rows, local_width)
        keys = jnp.dot(encoded, w_key, preferred_element_type=jnp.float32).astype(jnp.bfloat16)
        values = jnp.dot(encoded, w_value, preferred_element_type=jnp.float32).astype(
            jnp.bfloat16
        )
        return keys.reshape(shape), values.reshape(shape)

    kept_rows = [encode(piece) for piece in kept]
    passed_rows = [encode(piece) for piece in passed]
    always = jnp.ones((1,), jnp.int32)
    out = None
    for span in range(1, per_span):
        out = attend(
            span, per_span, always, queries, [k for k, _ in kept_rows],
            [v for _, v in kept_rows], out, per_span - 1, span - 1,
        )
    has_source = (my_index > 0).astype(jnp.int32).reshape(1)
    return attend(
        0, per_span, has_source, queries, [k for k, _ in passed_rows],
        [v for _, v in passed_rows], out, 1, 0,
    )


def solution(mesh):
    return jax.shard_map(
        step,
        mesh=mesh,
        in_specs=(
            P("dp", "seq", "mp"),
            P("seq", None, "mp"),
            P("dp", None, None, None),
            P("dp", None, None, None),
            P(),
            P(),
            P(None, "mp"),
            P("mp", None),
            P(None, "mp"),
            P(None, "mp"),
        ),
        out_specs=P("dp", "seq", "mp"),
        check_vma=False,
    )
```

```python
import functools

import jax
import jax.numpy as jnp
from jax import lax
from jax.experimental import pallas as pl
from jax.experimental.pallas import tpu as pltpu
from jax.sharding import PartitionSpec as P


HD = 128
MOST = 2
CHUNKS = 2

epsilon = 1e-06


def rms_scale(values, gain_values):
    return (
        values
        * lax.rsqrt(jnp.mean(values * values, axis=-1, keepdims=True) + epsilon)
        * gain_values
    )


def send_kernel(shards, requests, my_ref, owner_ref, row_ref, database_ref, *refs):
    out_refs, (wanted_ref, stage, in_sem, out_sem) = refs[:CHUNKS], refs[CHUNKS:]
    my_index = my_ref[0]
    rows = stage.shape[1] // CHUNKS

    def fetch(slot):
        return pltpu.make_async_copy(
            database_ref.at[wanted_ref[slot]], stage.at[slot], in_sem.at[slot]
        )

    def emit(slot, chunk):
        return pltpu.make_async_copy(
            stage.at[slot, pl.ds(chunk * rows, rows)],
            out_refs[chunk].at[slot],
            out_sem.at[chunk, slot],
        )

    @pl.loop(0, shards)
    def _(peer):
        for rank in range(MOST):
            wanted_ref[peer * MOST + rank] = 0
        rank = jnp.int32(0)
        for i in range(requests):
            mine = owner_ref[peer * requests + i] == my_index

            @pl.when(mine)
            def _():
                wanted_ref[peer * MOST + jnp.minimum(rank, MOST - 1)] = row_ref[
                    peer * requests + i
                ]

            rank = rank + mine.astype(jnp.int32)
        for rank in range(MOST):
            fetch(peer * MOST + rank).start()

    @pl.loop(0, shards * MOST)
    def _(slot):
        fetch(slot).wait()
        for chunk in range(CHUNKS):
            emit(slot, chunk).start()

    @pl.loop(0, shards * MOST)
    def _(slot):
        for chunk in range(CHUNKS):
            emit(slot, chunk).wait()


def gather_requests(database, owners, row_index, my_index, shards, requests):
    slots = shards * MOST
    block_len, width = database.shape[1:]
    piece = jax.ShapeDtypeStruct((slots, block_len // CHUNKS, width), database.dtype)
    return pl.pallas_call(
        functools.partial(send_kernel, shards, requests),
        out_shape=[piece] * CHUNKS,
        in_specs=[pl.BlockSpec(memory_space=pltpu.SMEM)] * 3
        + [pl.BlockSpec(memory_space=pl.ANY)],
        out_specs=[pl.BlockSpec(memory_space=pl.ANY)] * CHUNKS,
        scratch_shapes=[
            pltpu.SMEM((slots,), jnp.int32),
            pltpu.VMEM((slots, block_len, width), database.dtype),
            pltpu.SemaphoreType.DMA((slots,)),
            pltpu.SemaphoreType.DMA((CHUNKS, slots)),
        ],
        name="gather_requests",
    )(my_index, owners, row_index, database)


def pick_kernel(
    shards, requests, per_span, neigh, my_ref, owner_ref, arrived_ref, kept_ref, passed_ref,
    source_ref, count_ref, stage, in_sem, out_sem,
):
    my_index = my_ref[0]

    @pl.loop(0, shards)
    def _(shard):
        count_ref[shard] = 0

    for i in range(requests):
        owner = owner_ref[my_index * requests + i]
        rank = count_ref[owner]
        count_ref[owner] = rank + 1
        source_ref[i] = owner * MOST + jnp.minimum(rank, MOST - 1)

    def fetch(i):
        return pltpu.make_async_copy(
            arrived_ref.at[source_ref[i]], stage.at[i], in_sem.at[i]
        )

    def emit(i):
        sequence, span, place = (
            i // (per_span * neigh), (i // neigh) % per_span, i % neigh,
        )
        if span == per_span - 1:
            target = passed_ref.at[sequence * neigh + place]
        else:
            target = kept_ref.at[(sequence * (per_span - 1) + span) * neigh + place]
        return pltpu.make_async_copy(stage.at[i], target, out_sem.at[i])

    for i in range(requests):
        fetch(i).start()
    for i in range(requests):
        fetch(i).wait()
        emit(i).start()
    for i in range(requests):
        emit(i).wait()


def pick_blocks(arrived, owners, my_index, shards, requests, per_span, neigh):
    _, rows, width = arrived.shape
    sequences = requests // (per_span * neigh)
    passed_count = sequences * neigh
    return pl.pallas_call(
        functools.partial(pick_kernel, shards, requests, per_span, neigh),
        out_shape=[
            jax.ShapeDtypeStruct((requests - passed_count, rows, width), arrived.dtype),
            jax.ShapeDtypeStruct((passed_count, rows, width), arrived.dtype),
        ],
        in_specs=[pl.BlockSpec(memory_space=pltpu.SMEM)] * 2
        + [pl.BlockSpec(memory_space=pl.ANY)],
        out_specs=[pl.BlockSpec(memory_space=pl.ANY)] * 2,
        scratch_shapes=[
            pltpu.SMEM((requests,), jnp.int32),
            pltpu.SMEM((shards,), jnp.int32),
            pltpu.VMEM((requests, rows, width), arrived.dtype),
            pltpu.SemaphoreType.DMA((requests,)),
            pltpu.SemaphoreType.DMA((requests,)),
        ],
        name="pick_blocks",
    )(my_index, owners, arrived)


def attend_kernel(has_ref, query_ref, *refs):
    key_refs, value_refs = refs[:CHUNKS], refs[CHUNKS : 2 * CHUNKS]
    out_ref = refs[-1]
    keep = has_ref[0] > 0
    local_width = query_ref.shape[-1]
    heads = local_width // HD
    group = 4 if heads % 4 == 0 else 1
    span_len = query_ref.shape[1]

    def merged(part_refs, columns):
        pieces = []
        for ref in part_refs:
            piece = ref[0, :, :, columns]
            pieces.append(piece.reshape(-1, HD))
        return jnp.concatenate(pieces, axis=0)

    for first in range(0, heads, group):
        spots = [slice((first + i) * HD, (first + i + 1) * HD) for i in range(group)]
        scores = jnp.concatenate(
            [
                lax.dot_general(
                    query_ref[0, :, spot],
                    merged(key_refs, spot),
                    (((1,), (1,)), ((), ())),
                    preferred_element_type=jnp.float32,
                )
                for spot in spots
            ],
            axis=0,
        )
        scores = scores * HD ** (-0.5)
        weights = jnp.exp(scores - jnp.max(scores, axis=-1, keepdims=True))
        inverse = 1.0 / jnp.sum(weights, axis=-1, keepdims=True)
        weights = weights.astype(jnp.bfloat16)
        for i, spot in enumerate(spots):
            rows = slice(i * span_len, (i + 1) * span_len)
            attended = jnp.dot(
                weights[rows], merged(value_refs, spot), preferred_element_type=jnp.float32
            )
            out_ref[0, :, spot] = jnp.where(keep, attended * inverse[rows], 0.0).astype(
                out_ref.dtype
            )


def attend(span, per_span, has_source, queries, keys, values, out, group, offset):
    sequences, length, local_width = queries.shape
    span_len = length // per_span
    _, neigh, rows, _ = keys[0].shape
    query_spec = pl.BlockSpec((1, span_len, local_width), lambda q: (q, span, 0))
    block_spec = pl.BlockSpec(
        (1, neigh, rows, local_width), lambda q: (q * group + offset, 0, 0, 0)
    )
    fresh = out is None
    operands = [has_source, queries, *keys, *values, queries if fresh else out]
    keys_total = neigh * rows * CHUNKS * sequences
    return pl.pallas_call(
        attend_kernel,
        grid=(sequences,),
        out_shape=jax.ShapeDtypeStruct(queries.shape, queries.dtype),
        in_specs=[pl.BlockSpec(memory_space=pltpu.SMEM), query_spec]
        + [block_spec] * (2 * CHUNKS)
        + [pl.BlockSpec(memory_space=pl.ANY)],
        out_specs=query_spec,
        input_output_aliases={} if fresh else {len(operands) - 1: 0},
        cost_estimate=pl.CostEstimate(
            flops=4 * keys_total * span_len * local_width,
            bytes_accessed=4 * keys_total * local_width,
            transcendentals=keys_total * span_len * (local_width // HD),
        ),
        name="attend",
    )(*operands)


def join_kernel(me_ref, gain_ref, *refs):
    held_refs, (full_ref, normed_ref) = refs[:-2], refs[-2:]
    peers, width = len(held_refs), held_refs[0].shape[-1]
    pieces = [ref[...].astype(jnp.float32) for ref in held_refs]
    squares = sum(jnp.sum(piece * piece, axis=-1, keepdims=True) for piece in pieces)
    scale = lax.rsqrt(squares / (width * peers) + epsilon)
    for by in range(peers):
        owner = lax.rem(me_ref[0] - by + peers, peers)
        columns = pl.ds(pl.multiple_of(owner * width, width), width)
        full_ref[:, columns] = held_refs[by][...]
        normed_ref[:, columns] = (pieces[by] * scale * gain_ref[:, columns]).astype(
            normed_ref.dtype
        )


def joined(held, gain, tile):
    peers = len(held)
    me = lax.axis_index("mp").astype(jnp.int32).reshape(1)
    rows, width = held[0].shape
    full = jax.ShapeDtypeStruct((rows, width * peers), held[0].dtype)
    full_spec = pl.BlockSpec((tile, width * peers), lambda i: (i, 0))
    return pl.pallas_call(
        join_kernel,
        grid=(rows // tile,),
        out_shape=[full, full],
        in_specs=[
            pl.BlockSpec(memory_space=pltpu.SMEM),
            pl.BlockSpec((1, width * peers), lambda i: (0, 0)),
        ]
        + [pl.BlockSpec((tile, width), lambda i: (i, 0))] * peers,
        out_specs=[full_spec, full_spec],
        cost_estimate=pl.CostEstimate(
            flops=6 * rows * width * peers, bytes_accessed=6 * rows * width * peers,
            transcendentals=rows,
        ),
        name="joined",
    )(me, gain.reshape(1, -1), *held)


def project_kernel(gain_ref, w_key_ref, w_value_ref, *refs):
    term_refs, (key_ref, value_ref, encoded_ref) = refs[:-3], refs[-3:]

    @pl.when(pl.program_id(0) == 0)
    def _():
        total = term_refs[0][...].astype(jnp.float32)
        for ref in term_refs[1:]:
            total = total + ref[...].astype(jnp.float32)
        encoded_ref[...] = rms_scale(total, gain_ref[...]).astype(encoded_ref.dtype)

    for weight_ref, out_ref in ((w_key_ref, key_ref), (w_value_ref, value_ref)):
        out_ref[...] = jnp.dot(
            encoded_ref[...], weight_ref[...], preferred_element_type=jnp.float32
        ).astype(out_ref.dtype)


def projected(terms, gain, w_key, w_value):
    rows, width = terms[0].shape
    columns = w_key.shape[1]
    tile = 512 if columns % 512 == 0 else columns
    term_spec = pl.BlockSpec((rows, width), lambda i: (0, 0))
    weight_spec = pl.BlockSpec((width, tile), lambda i: (0, i))
    out_spec = pl.BlockSpec((rows, tile), lambda i: (0, i))
    out = jax.ShapeDtypeStruct((rows, columns), jnp.bfloat16)
    return pl.pallas_call(
        project_kernel,
        grid=(columns // tile,),
        out_shape=[out, out],
        in_specs=[pl.BlockSpec((1, width), lambda i: (0, 0)), weight_spec, weight_spec]
        + [term_spec] * len(terms),
        out_specs=[out_spec, out_spec],
        scratch_shapes=[pltpu.VMEM((rows, width), jnp.bfloat16)],
        cost_estimate=pl.CostEstimate(
            flops=4 * rows * width * columns, bytes_accessed=4 * (width + rows) * columns,
            transcendentals=rows,
        ),
        name="projected",
    )(gain.reshape(1, -1), w_key, w_value, *terms)


def swapped(array, axis, by):
    peers = lax.axis_size(axis)
    return lax.ppermute(array, axis, [(i, (i + by) % peers) for i in range(peers)])


def passed_along(array, axis, by):
    peers = lax.axis_size(axis)
    pairs = [(i, i + by) for i in range(peers) if 0 <= i + by < peers]
    return lax.ppermute(array, axis, pairs)


def step(queries, database, owner_ids, row_ids, pre_gain, out_gain, w_in, w_out, w_key, w_value):
    shards = lax.axis_size("seq")
    my_index = lax.axis_index("seq")
    peers = lax.axis_size("mp")
    sequences, _, local_width = queries.shape
    slot_count, neigh = owner_ids.shape[2:]
    per_span = slot_count // sequences
    requests = slot_count * neigh
    owners = owner_ids.reshape(-1)
    row_index = row_ids.reshape(-1)
    mine = my_index.astype(jnp.int32).reshape(1)
    sending = gather_requests(database, owners, row_index, mine, shards, requests)
    kept, passed = [], []
    for chunk in range(CHUNKS):
        piece = sending[chunk]
        arrived = lax.all_to_all(
            piece.reshape((shards, MOST) + piece.shape[1:]),
            "seq",
            split_axis=0,
            concat_axis=0,
            tiled=True,
        ).reshape(piece.shape)
        stay, leave = pick_blocks(arrived, owners, mine, shards, requests, per_span, neigh)
        kept.append(stay)
        passed.append(passed_along(leave, "seq", 1))

    def encode(own):
        rows = own.shape[1]
        own = own.reshape(-1, own.shape[-1])
        held = [own] + [swapped(own, "mp", by) for by in range(1, peers)]
        blocks, normed = joined(held, pre_gain, neigh * rows)
        hidden = jax.nn.gelu(
            jnp.dot(normed, w_in, preferred_element_type=jnp.float32)
        ).astype(jnp.bfloat16)
        partial = jnp.dot(hidden, w_out, preferred_element_type=jnp.float32).astype(
            jnp.bfloat16
        )
        others = [swapped(partial, "mp", by) for by in range(1, peers)]
        keys, values = projected([blocks, partial, *others], out_gain, w_key, w_value)
        shape = (-1, neigh, rows, local_width)
        return keys.reshape(shape), values.reshape(shape)

    kept_rows = [encode(piece) for piece in kept]
    passed_rows = [encode(piece) for piece in passed]
    always = jnp.ones((1,), jnp.int32)
    out = None
    for span in range(1, per_span):
        out = attend(
            span, per_span, always, queries, [k for k, _ in kept_rows],
            [v for _, v in kept_rows], out, per_span - 1, span - 1,
        )
    has_source = (my_index > 0).astype(jnp.int32).reshape(1)
    return attend(
        0, per_span, has_source, queries, [k for k, _ in passed_rows],
        [v for _, v in passed_rows], out, 1, 0,
    )


def solution(mesh):
    return jax.shard_map(
        step,
        mesh=mesh,
        in_specs=(
            P("dp", "seq", "mp"),
            P("seq", None, "mp"),
            P("dp", None, None, None),
            P("dp", None, None, None),
            P(),
            P(),
            P(None, "mp"),
            P("mp", None),
            P(None, "mp"),
            P(None, "mp"),
        ),
        out_specs=P("dp", "seq", "mp"),
        check_vma=False,
    )
```
